256 devices in a mesh: wide: 32 (over z, x), narrow: 8 (over y, core).
Axes of the slice: x: 4, y: 4, z: 8, core: 2. Of those that a mesh axis runs over, the one named last changes fastest.
Arguments:
- cube: bfloat16 [256, 1536, 224], P('narrow', 'wide')
Outputs:
- restored: bfloat16 [256, 1536, 224], P('narrow', 'wide')
- projector: float32 [224, 224], replicated
All inputs are finite; a program needn't handle non-finite values.
Results may differ from the reference program's by a relative error of at most 0.0034.
Values may be sent and summed in bfloat16 or wider, within the bound.
A program may use at most 64 MiB of HBM per device.

```python
import jax
import jax.numpy as jnp
from jax import lax

TILE_ROWS = 32
BANDS = 224
RANK = 16
POWER_ITERS = 4
TV_ITERS = 3
HEIGHT = 256
WIDTH = 1536
N_NARROW = 8


def draw_cube(key, part):
    key_abund, key_spec, key_noise, key_phase = jax.random.split(key, 4)
    sources = 3 * RANK
    abund = jax.random.normal(key_abund, (HEIGHT, WIDTH, sources), jnp.float32)
    noise = 0.3 * jax.random.normal(key_noise, (HEIGHT, WIDTH, BANDS), jnp.float32)
    spectra = jax.random.normal(key_spec, (sources, BANDS), jnp.float32)
    order = jnp.arange(sources, dtype=jnp.float32)
    spectra = spectra * jnp.exp(-0.07 * order)[:, None]
    phases = jax.random.uniform(key_phase, (2, sources), jnp.float32, 0.0, 1.0)
    rows = jnp.arange(HEIGHT, dtype=jnp.float32) / HEIGHT
    cols = jnp.arange(WIDTH, dtype=jnp.float32) / WIDTH
    row_mod = jnp.exp(0.5 * jnp.cos(2.0 * jnp.pi * (rows[:, None] + phases[0][None, :])))
    col_mod = jnp.exp(0.5 * jnp.cos(2.0 * jnp.pi * (cols[:, None] + phases[1][None, :])))
    abund = abund * row_mod[:, None, :] * col_mod[None, :, :]
    mixed = jnp.einsum('hwr,rb->hwb', abund, spectra, precision=lax.Precision.HIGHEST)
    spread = jnp.exp(jnp.log(3.0) * (rows[:, None] + cols[None, :]) * 0.5)
    return (0.25 * spread[:, :, None] * (mixed + noise)).astype(jnp.bfloat16)


def setup_inputs(seed: int = 0) -> dict:
    seeds = jax.random.split(jax.random.key(seed), 2)
    return {
        "cube": draw_cube(jax.random.fold_in(seeds[1], 71), 0),
    }


hi_prec = lax.Precision.HIGHEST

def smooth_step(field, fitted, grow, gcol, height, width):
    mask_x = ((grow >= 0) & (grow + 1 < height)).astype(jnp.float32)
    mask_y = ((gcol >= 0) & (gcol + 1 < width)).astype(jnp.float32)
    corner = field[:-1, :-1]
    grad_x = (field[1:, :-1] - corner) * mask_x[:-1, None, None]
    grad_y = (field[:-1, 1:] - corner) * mask_y[None, :-1, None]
    magnitude = jnp.sqrt(grad_x * grad_x + grad_y * grad_y + 0.25)
    flow_x = grad_x / magnitude
    flow_y = grad_y / magnitude
    diverg = flow_x[1:, 1:] - flow_x[:-1, 1:] + flow_y[1:, 1:] - flow_y[1:, :-1]
    centre = field[1:-1, 1:-1]
    return centre - 0.5 * (centre - fitted[1:-1, 1:-1] - 0.5 * diverg)

def subspace(gram):
    bands = lax.broadcasted_iota(jnp.float32, (BANDS, RANK), 0)
    cols = lax.broadcasted_iota(jnp.float32, (BANDS, RANK), 1)
    basis = jnp.cos(jnp.pi * (bands + 0.5) * cols / BANDS)
    for step in range(POWER_ITERS):
        grown = jnp.dot(gram, basis, precision=hi_prec)
        inner = jnp.dot(grown.T, grown, precision=hi_prec)
        lower = jnp.linalg.cholesky(inner)
        basis = jax.scipy.linalg.solve_triangular(lower, grown.T, lower=True).T
    return basis

def reference(cube):
    flat = cube.reshape(HEIGHT * WIDTH, BANDS)
    gram = lax.dot_general(flat.astype(jnp.float32), flat.astype(jnp.float32), (((0,), (0,)), ((), ())), preferred_element_type=jnp.float32)
    gram = gram / (HEIGHT * WIDTH)
    basis = subspace(gram)
    projector = jnp.dot(basis, basis.T, precision=hi_prec)
    basis_low = basis.astype(jnp.bfloat16)
    depth = TV_ITERS
    padded = jnp.pad(cube, ((depth, depth), (depth, depth), (0, 0)))
    gcol = jnp.arange(WIDTH + 2 * depth, dtype=jnp.int32) - depth

    def one_block(index):
        start = (index * TILE_ROWS).astype(jnp.int32)
        block = lax.dynamic_slice_in_dim(padded, start, TILE_ROWS + 2 * depth, 0)
        loading = jnp.einsum('hwb,br->hwr', block.astype(jnp.float32), basis_low.astype(jnp.float32), preferred_element_type=jnp.float32)
        fitted = jnp.einsum('hwr,br->hwb', loading, basis, precision=hi_prec)
        grow = start - depth + jnp.arange(TILE_ROWS + 2 * depth, dtype=jnp.int32)
        field = fitted
        rows, cols = (grow, gcol)
        for step in range(TV_ITERS):
            field = smooth_step(field, fitted, rows, cols, HEIGHT, WIDTH)
            fitted = fitted[1:-1, 1:-1]
            rows, cols = (rows[1:-1], cols[1:-1])
        return field.astype(jnp.bfloat16)
    blocks = lax.map(one_block, jnp.arange(N_NARROW, dtype=jnp.int32))
    restored = blocks.reshape(HEIGHT, WIDTH, BANDS)
    return (restored, projector)
```

```python
import functools

import jax
import jax.numpy as jnp
import numpy as np
from jax import lax
from jax.experimental import pallas as pl
from jax.experimental.pallas import tpu as pltpu
from jax.sharding import PartitionSpec as P

TILE_ROWS = 32
TILE_COLS = 48
PIXELS = TILE_ROWS * TILE_COLS
BANDS = 224
RANK = 16
POWER_ITERS = 4
TV_ITERS = 3
CHIPS_X = 4
CHIPS_Z = 8
N_NARROW = 8
N_WIDE = CHIPS_X * CHIPS_Z
PLANE = CHIPS_X * N_NARROW
TOTAL_PIXELS = PIXELS * N_NARROW * N_WIDE
DEPTH = TV_ITERS
BORDER = DEPTH * TILE_COLS
SIDE = TILE_ROWS * 4
TOP, BOTTOM, LEFT, RIGHT, CORNER = 0, BORDER, 2 * BORDER, 2 * BORDER + SIDE, 2 * BORDER + 2 * SIDE
HALO = CORNER + 64
EXT_ROWS = TILE_ROWS + 2 * DEPTH
EXT_COLS = TILE_COLS + 16

MESH = pl.DeviceIdType.MESH
HIGHEST = lax.Precision.HIGHEST
F32 = jnp.float32
BF16 = jnp.bfloat16
TN = (((0,), (0,)), ((), ()))
NT = (((1,), (1,)), ((), ()))


def select_columns(pixels, first):
    shape = (SIDE, TILE_ROWS * 16)
    want = lax.broadcasted_iota(jnp.int32, shape, 0)
    have = lax.broadcasted_iota(jnp.int32, shape, 1)
    pick = (have == (want // 4) * 16 + want % 4 + first).astype(F32).astype(BF16)
    flat = pixels.reshape(TILE_ROWS * 16, BANDS)
    return jnp.dot(pick, flat, preferred_element_type=F32).astype(BF16)


def exchange_kernel(
    cube_ref, gram_ref, halo_ref,
    tile, packed, around, own, along, summed, edge_l, edge_r, halo,
    load_sem, send_sem, recv_sem, halo_send, halo_recv,
):
    wide = lax.axis_index("wide")
    narrow = lax.axis_index("narrow")
    z = wide // CHIPS_X
    x = wide % CHIPS_X
    block = x * N_NARROW + narrow

    load = pltpu.make_async_copy(cube_ref, tile, load_sem)
    load.start()

    def in_plane(step):
        other = (block + step) % PLANE
        return (z * CHIPS_X + other // N_NARROW, other % N_NARROW), other

    def on_line(step):
        return (((z + step) % CHIPS_Z) * CHIPS_X + x, narrow)

    def beside(dr, dc):
        return ((wide + dc + N_WIDE) % N_WIDE, (narrow + dr + N_NARROW) % N_NARROW)

    barrier = pltpu.get_barrier_semaphore()

    @pl.loop(1, PLANE)
    def _(step):
        pl.semaphore_signal(barrier, inc=1, device_id=in_plane(step)[0], device_id_type=MESH)

    @pl.loop(1, CHIPS_Z)
    def _(step):
        pl.semaphore_signal(barrier, inc=1, device_id=on_line(step), device_id_type=MESH)

    for dr in (-1, 0, 1):
        for dc in (-1, 0, 1):
            if dr or dc:
                pl.semaphore_signal(barrier, inc=1, device_id=beside(dr, dc), device_id_type=MESH)

    load.wait()
    values = tile[...]
    local = lax.dot_general(values, values, TN, preferred_element_type=F32)
    row = lax.broadcasted_iota(jnp.int32, (128, 128), 0)
    col = lax.broadcasted_iota(jnp.int32, (128, 128), 1)
    first = local[:128, :128]
    cross = jnp.concatenate([local[:128, 128:], jnp.zeros((128, 32), F32)], axis=1)
    last = jnp.concatenate([local[128:, 128:], jnp.zeros((96, 32), F32)], axis=1)
    last = jnp.concatenate([last, jnp.zeros((32, 128), F32)], axis=0)
    diagonal = jnp.sum(jnp.where(row == col, last, 0.0), axis=1, keepdims=True)
    packed[:16] = jnp.where(row <= col, first, last).reshape(16, 8, 128)
    packed[16:] = jnp.where(col == 96, diagonal, cross).reshape(16, 8, 128)

    pl.semaphore_wait(barrier, PLANE - 1 + CHIPS_Z - 1 + 8)

    @pl.loop(1, PLANE)
    def _(step):
        device, other = in_plane(step)
        pltpu.make_async_remote_copy(
            src_ref=packed.at[other], dst_ref=around.at[step - 1],
            send_sem=send_sem.at[0], recv_sem=recv_sem.at[0],
            device_id=device, device_id_type=MESH,
        ).start()

    grid = values.reshape(TILE_ROWS, TILE_COLS, BANDS)
    edge_l[...] = select_columns(grid[:, :16], 0)
    edge_r[...] = select_columns(grid[:, 32:], 12)
    pieces = (
        (-1, 0, tile.at[pl.ds(0, BORDER)], BOTTOM, BORDER),
        (1, 0, tile.at[pl.ds(PIXELS - BORDER, BORDER)], TOP, BORDER),
        (0, -1, edge_l, RIGHT, SIDE),
        (0, 1, edge_r, LEFT, SIDE),
        (-1, -1, edge_l.at[pl.ds(0, 16)], CORNER + 48, 16),
        (1, -1, edge_l.at[pl.ds(SIDE - 16, 16)], CORNER + 16, 16),
        (-1, 1, edge_r.at[pl.ds(0, 16)], CORNER + 32, 16),
        (1, 1, edge_r.at[pl.ds(SIDE - 16, 16)], CORNER, 16),
    )
    borders = []
    for index, (dr, dc, source, at, size) in enumerate(pieces):
        copy = pltpu.make_async_remote_copy(
            src_ref=source, dst_ref=halo.at[pl.ds(at, size)],
            send_sem=halo_send.at[index], recv_sem=halo_recv.at[index],
            device_id=beside(dr, dc), device_id_type=MESH,
        )
        copy.start()
        borders.append(copy)

    def wait_for(ref, count, sem):
        part = ref.at[pl.ds(0, count)]
        pltpu.make_async_copy(part, part, sem).wait()

    wait_for(around, PLANE - 1, recv_sem.at[0])
    total = packed[block]
    for step in range(PLANE - 1):
        total = total + around[step]
    own[...] = total
    along[z] = total

    @pl.loop(1, CHIPS_Z)
    def _(step):
        pltpu.make_async_remote_copy(
            src_ref=own, dst_ref=along.at[z],
            send_sem=send_sem.at[1], recv_sem=recv_sem.at[1],
            device_id=on_line(step), device_id_type=MESH,
        ).start()

    wait_for(along, CHIPS_Z - 1, recv_sem.at[1])
    total = along[0]
    for step in range(1, CHIPS_Z):
        total = total + along[step]
    summed[block] = total

    @pl.loop(1, PLANE)
    def _(step):
        device, other = in_plane(step)
        pltpu.make_async_remote_copy(
            src_ref=summed.at[block], dst_ref=summed.at[block],
            send_sem=send_sem.at[2], recv_sem=recv_sem.at[2],
            device_id=device, device_id_type=MESH,
        ).start()

    for copy in borders:
        copy.wait_recv()
    halo_ref[...] = halo[...]
    wait_for(summed, PLANE - 1, recv_sem.at[2])
    gram_ref[...] = summed[...].reshape(256, 128)
    wait_for(packed, PLANE - 1, send_sem.at[0])
    wait_for(along, CHIPS_Z - 1, send_sem.at[1])
    wait_for(summed, PLANE - 1, send_sem.at[2])
    for copy in borders:
        copy.wait_send()


def exchange(cube):
    return pl.pallas_call(
        exchange_kernel,
        out_shape=(
            jax.ShapeDtypeStruct((256, 128), F32),
            jax.ShapeDtypeStruct((HALO, BANDS), BF16),
        ),
        in_specs=[pl.BlockSpec(memory_space=pl.ANY)],
        out_specs=(pl.BlockSpec(memory_space=pltpu.VMEM), pl.BlockSpec(memory_space=pltpu.VMEM)),
        scratch_shapes=[
            pltpu.VMEM((PIXELS, BANDS), BF16),
            pltpu.VMEM((PLANE, 8, 128), F32),
            pltpu.VMEM((PLANE, 8, 128), F32),
            pltpu.VMEM((8, 128), F32),
            pltpu.VMEM((CHIPS_Z, 8, 128), F32),
            pltpu.VMEM((PLANE, 8, 128), F32),
            pltpu.VMEM((SIDE, BANDS), BF16),
            pltpu.VMEM((SIDE, BANDS), BF16),
            pltpu.VMEM((HALO, BANDS), BF16),
            pltpu.SemaphoreType.DMA,
            pltpu.SemaphoreType.DMA((3,)),
            pltpu.SemaphoreType.DMA((3,)),
            pltpu.SemaphoreType.DMA((8,)),
            pltpu.SemaphoreType.DMA((8,)),
        ],
        compiler_params=pltpu.CompilerParams(collective_id=0, has_side_effects=True),
    )(cube)


def split(values):
    high = values.astype(BF16)
    return high, (values - high.astype(F32)).astype(BF16)


def subspace(packed, start):
    row = lax.broadcasted_iota(jnp.int32, (128, 128), 0)
    col = lax.broadcasted_iota(jnp.int32, (128, 128), 1)
    packed = packed * (1.0 / TOTAL_PIXELS)
    mixed, cross = packed[:128], packed[128:]
    flipped = mixed.T
    first = jnp.where(row <= col, mixed, flipped)
    inside = (row < 96) & (col < 96)
    last = jnp.where(inside, jnp.where(row > col, mixed, flipped), 0.0)
    last = jnp.where(inside & (row == col), cross[:, 96:97], last)
    cross = jnp.where(col < 96, cross, 0.0)
    gram = jnp.concatenate(
        [jnp.concatenate([first, cross], axis=1), jnp.concatenate([cross.T, last], axis=1)], axis=0
    )
    rank_row = lax.broadcasted_iota(jnp.int32, (RANK, 1), 0)
    basis = start
    for _ in range(POWER_ITERS):
        grown = jnp.dot(basis, gram, precision=HIGHEST, preferred_element_type=F32)
        inner = lax.dot_general(grown, grown, NT, precision=HIGHEST, preferred_element_type=F32)
        scale = jnp.zeros((RANK, 1), F32)
        for step in range(RANK):
            pivot = inner[step : step + 1, step : step + 1]
            scale = jnp.where(rank_row == step, lax.rsqrt(pivot), scale)
            if step < RANK - 1:
                factor = jnp.where(rank_row > step, inner[:, step : step + 1] / pivot, 0.0)
                inner = inner - factor * inner[step : step + 1, :]
                grown = grown - factor * grown[step : step + 1, :]
        basis = grown * scale
    return basis


def smooth_kernel(gram_ref, halo_ref, cube_ref, start_ref, out_ref, proj_ref, u0, u1, u2, flow):
    wide = lax.axis_index("wide")
    narrow = lax.axis_index("narrow")
    basis = subspace(gram_ref[...], start_ref[...])
    proj_ref[...] = lax.dot_general(
        basis, basis, TN, precision=HIGHEST, preferred_element_type=F32
    )[:BANDS, :BANDS]
    low = basis.astype(BF16).astype(F32)
    fit = 4.0 * lax.dot_general(low, basis, TN, precision=HIGHEST, preferred_element_type=F32)
    high, rest = split(fit[:BANDS])

    def fitted(pixels):
        return jnp.dot(pixels, high, preferred_element_type=F32) + jnp.dot(
            pixels, rest, preferred_element_type=F32
        )

    def put(values, rows, row, col, count):
        for half in range(2):
            part = values[:, half * 128 : (half + 1) * 128]
            for r in range(rows):
                u0[half, row + r, col : col + count, :] = part[r * count : (r + 1) * count]

    put(fitted(halo_ref[TOP : TOP + BORDER]), DEPTH, 0, 8, TILE_COLS)
    put(fitted(halo_ref[BOTTOM : BOTTOM + BORDER]), DEPTH, DEPTH + TILE_ROWS, 8, TILE_COLS)
    put(fitted(halo_ref[LEFT : LEFT + SIDE]), TILE_ROWS, DEPTH, 4, 4)
    put(fitted(halo_ref[RIGHT : RIGHT + SIDE]), TILE_ROWS, DEPTH, 8 + TILE_COLS, 4)
    corners = fitted(halo_ref[CORNER : CORNER + 64])
    put(corners[4:16], DEPTH, 0, 4, 4)
    put(corners[20:32], DEPTH, 0, 8 + TILE_COLS, 4)
    put(corners[32:44], DEPTH, DEPTH + TILE_ROWS, 4, 4)
    put(corners[48:60], DEPTH, DEPTH + TILE_ROWS, 8 + TILE_COLS, 4)

    @pl.loop(0, TILE_ROWS // 4)
    def _(index):
        at = pl.multiple_of(index * (4 * TILE_COLS), 4 * TILE_COLS)
        values = fitted(cube_ref[pl.ds(at, 4 * TILE_COLS), :])
        put(values, 4, DEPTH + index * 4, 8, TILE_COLS)

    stages = (u0, u1, u2)
    for turn in range(TV_ITERS):
        here = stages[turn]

        @pl.when(narrow == 0)
        def _():
            here[:, DEPTH - 1] = here[:, DEPTH]

        @pl.when(narrow == N_NARROW - 1)
        def _():
            here[:, DEPTH + TILE_ROWS] = here[:, DEPTH + TILE_ROWS - 1]

        @pl.when(wide == 0)
        def _():
            here[:, :, 7:8, :] = here[:, :, 8:9, :]

        @pl.when(wide == N_WIDE - 1)
        def _():
            here[:, :, 8 + TILE_COLS : 9 + TILE_COLS, :] = here[:, :, 7 + TILE_COLS : 8 + TILE_COLS, :]

        last = turn == TV_ITERS - 1
        for half in range(2):

            def flows(row):
                middle = here[half, row, 0:EXT_COLS, :]
                gx = here[half, row + 1, 0:EXT_COLS, :] - middle
                gy = here[half, row, 1 : EXT_COLS + 1, :] - middle
                scale = lax.rsqrt(gx * gx + gy * gy + 4.0)
                return middle, gx * scale, gy * scale

            def line(row, above):
                middle, px, py = flows(row)
                flow[8 : 8 + EXT_COLS, :] = py
                change = px - above + (py - flow[7 : 7 + EXT_COLS, :])
                if turn == 0:
                    value = middle + change
                else:
                    value = 0.5 * (middle + u0[half, row, 0:EXT_COLS, :]) + change
                if last:
                    width = 128 if half == 0 else BANDS - 128
                    at = pl.multiple_of((row - DEPTH) * TILE_COLS, TILE_COLS)
                    out_ref[pl.ds(at, TILE_COLS), half * 128 : half * 128 + width] = (
                        0.25 * value[8 : 8 + TILE_COLS, :width]
                    ).astype(BF16)
                else:
                    stages[turn + 1][half, row, 0:EXT_COLS, :] = value
                return px

            lax.fori_loop(turn + 1, EXT_ROWS - 1 - turn, line, flows(turn)[1])


def smooth(gram, halo, cube, start):
    vmem = pl.BlockSpec(memory_space=pltpu.VMEM)
    field = pltpu.VMEM((2, EXT_ROWS, EXT_COLS + 8, 128), F32)
    return pl.pallas_call(
        smooth_kernel,
        out_shape=(
            jax.ShapeDtypeStruct((PIXELS, BANDS), BF16),
            jax.ShapeDtypeStruct((BANDS, BANDS), F32),
        ),
        in_specs=[vmem] * 4,
        out_specs=(vmem, vmem),
        scratch_shapes=[field, field, field, pltpu.VMEM((EXT_COLS + 16, 128), F32)],
    )(gram, halo, cube, start)


def first_basis():
    bands = np.arange(256)[None, :]
    cols = np.arange(RANK)[:, None]
    values = np.cos(np.pi * (bands + 0.5) * cols / BANDS)
    return np.where(bands < BANDS, values, 0.0).astype(np.float32)


def body(cube):
    flat = cube.reshape(PIXELS, BANDS)
    gram, halo = exchange(flat)
    restored, projector = smooth(gram, halo, flat, jnp.asarray(first_basis()))
    return restored.reshape(TILE_ROWS, TILE_COLS, BANDS), projector


def solution(mesh):
    return jax.shard_map(
        body,
        mesh=mesh,
        in_specs=(P("narrow", "wide", None),),
        out_specs=(P("narrow", "wide", None), P()),
        check_vma=False,
    )
```

```python
import functools

import jax
import jax.numpy as jnp
import numpy as np
from jax import lax
from jax.experimental import pallas as pl
from jax.experimental.pallas import tpu as pltpu
from jax.sharding import PartitionSpec as P

TILE_ROWS = 32
TILE_COLS = 48
PIXELS = TILE_ROWS * TILE_COLS
BANDS = 224
RANK = 16
POWER_ITERS = 4
TV_ITERS = 3
CHIPS_X = 4
CHIPS_Z = 8
N_NARROW = 8
N_WIDE = CHIPS_X * CHIPS_Z
PLANE = CHIPS_X * N_NARROW
TOTAL_PIXELS = PIXELS * N_NARROW * N_WIDE
DEPTH = TV_ITERS
BORDER = DEPTH * TILE_COLS
SIDE = TILE_ROWS * 4
TOP, BOTTOM, LEFT, RIGHT, CORNER = 0, BORDER, 2 * BORDER, 2 * BORDER + SIDE, 2 * BORDER + 2 * SIDE
HALO = CORNER + 64
EXT_ROWS = TILE_ROWS + 2 * DEPTH
EXT_COLS = TILE_COLS + 16

MESH = pl.DeviceIdType.MESH
HIGHEST = lax.Precision.HIGHEST
F32 = jnp.float32
BF16 = jnp.bfloat16
TN = (((0,), (0,)), ((), ()))
NT = (((1,), (1,)), ((), ()))


def select_columns(pixels, first):
    shape = (SIDE, TILE_ROWS * 16)
    want = lax.broadcasted_iota(jnp.int32, shape, 0)
    have = lax.broadcasted_iota(jnp.int32, shape, 1)
    pick = (have == (want // 4) * 16 + want % 4 + first).astype(F32).astype(BF16)
    flat = pixels.reshape(TILE_ROWS * 16, BANDS)
    return jnp.dot(pick, flat, preferred_element_type=F32).astype(BF16)


def exchange_kernel(
    cube_ref, gram_ref, halo_ref,
    tile, packed, around, own, along, summed, edge_l, edge_r, halo,
    load_sem, send_sem, recv_sem, halo_send, halo_recv,
):
    wide = lax.axis_index("wide")
    narrow = lax.axis_index("narrow")
    z = wide // CHIPS_X
    x = wide % CHIPS_X
    block = x * N_NARROW + narrow

    load = pltpu.make_async_copy(cube_ref, tile, load_sem)
    load.start()

    def in_plane(step):
        other = (block + step) % PLANE
        return (z * CHIPS_X + other // N_NARROW, other % N_NARROW), other

    def on_line(step):
        return (((z + step) % CHIPS_Z) * CHIPS_X + x, narrow)

    def beside(dr, dc):
        return ((wide + dc + N_WIDE) % N_WIDE, (narrow + dr + N_NARROW) % N_NARROW)

    barrier = pltpu.get_barrier_semaphore()

    @pl.loop(1, PLANE)
    def _(step):
        pl.semaphore_signal(barrier, inc=1, device_id=in_plane(step)[0], device_id_type=MESH)

    @pl.loop(1, CHIPS_Z)
    def _(step):
        pl.semaphore_signal(barrier, inc=1, device_id=on_line(step), device_id_type=MESH)

    for dr in (-1, 0, 1):
        for dc in (-1, 0, 1):
            if dr or dc:
                pl.semaphore_signal(barrier, inc=1, device_id=beside(dr, dc), device_id_type=MESH)

    load.wait()
    values = tile[...]
    local = lax.dot_general(values, values, TN, preferred_element_type=F32)
    row = lax.broadcasted_iota(jnp.int32, (128, 128), 0)
    col = lax.broadcasted_iota(jnp.int32, (128, 128), 1)
    first = local[:128, :128]
    cross = jnp.concatenate([local[:128, 128:], jnp.zeros((128, 32), F32)], axis=1)
    last = jnp.concatenate([local[128:, 128:], jnp.zeros((96, 32), F32)], axis=1)
    last = jnp.concatenate([last, jnp.zeros((32, 128), F32)], axis=0)
    diagonal = jnp.sum(jnp.where(row == col, last, 0.0), axis=1, keepdims=True)
    packed[:16] = jnp.where(row <= col, first, last).reshape(16, 8, 128)
    packed[16:] = jnp.where(col == 96, diagonal, cross).reshape(16, 8, 128)

    pl.semaphore_wait(barrier, PLANE - 1 + CHIPS_Z - 1 + 8)

    @pl.loop(1, PLANE)
    def _(step):
        device, other = in_plane(step)
        pltpu.make_async_remote_copy(
            src_ref=packed.at[other], dst_ref=around.at[step - 1],
            send_sem=send_sem.at[0], recv_sem=recv_sem.at[0],
            device_id=device, device_id_type=MESH,
        ).start()

    grid = values.reshape(TILE_ROWS, TILE_COLS, BANDS)
    edge_l[...] = select_columns(grid[:, :16], 0)
    edge_r[...] = select_columns(grid[:, 32:], 12)
    pieces = (
        (-1, 0, tile.at[pl.ds(0, BORDER)], BOTTOM, BORDER),
        (1, 0, tile.at[pl.ds(PIXELS - BORDER, BORDER)], TOP, BORDER),
        (0, -1, edge_l, RIGHT, SIDE),
        (0, 1, edge_r, LEFT, SIDE),
        (-1, -1, edge_l.at[pl.ds(0, 16)], CORNER + 48, 16),
        (1, -1, edge_l.at[pl.ds(SIDE - 16, 16)], CORNER + 16, 16),
        (-1, 1, edge_r.at[pl.ds(0, 16)], CORNER + 32, 16),
        (1, 1, edge_r.at[pl.ds(SIDE - 16, 16)], CORNER, 16),
    )
    borders = []
    for index, (dr, dc, source, at, size) in enumerate(pieces):
        copy = pltpu.make_async_remote_copy(
            src_ref=source, dst_ref=halo.at[pl.ds(at, size)],
            send_sem=halo_send.at[index], recv_sem=halo_recv.at[index],
            device_id=beside(dr, dc), device_id_type=MESH,
        )
        copy.start()
        borders.append(copy)

    def wait_for(ref, count, sem):
        part = ref.at[pl.ds(0, count)]
        pltpu.make_async_copy(part, part, sem).wait()

    wait_for(around, PLANE - 1, recv_sem.at[0])
    total = packed[block]
    for step in range(PLANE - 1):
        total = total + around[step]
    own[...] = total
    along[z] = total

    @pl.loop(1, CHIPS_Z)
    def _(step):
        pltpu.make_async_remote_copy(
            src_ref=own, dst_ref=along.at[z],
            send_sem=send_sem.at[1], recv_sem=recv_sem.at[1],
            device_id=on_line(step), device_id_type=MESH,
        ).start()

    wait_for(along, CHIPS_Z - 1, recv_sem.at[1])
    total = along[0]
    for step in range(1, CHIPS_Z):
        total = total + along[step]
    summed[block] = total

    @pl.loop(1, PLANE)
    def _(step):
        device, other = in_plane(step)
        pltpu.make_async_remote_copy(
            src_ref=summed.at[block], dst_ref=summed.at[block],
            send_sem=send_sem.at[2], recv_sem=recv_sem.at[2],
            device_id=device, device_id_type=MESH,
        ).start()

    for copy in borders:
        copy.wait_recv()
    halo_ref[...] = halo[...]
    wait_for(summed, PLANE - 1, recv_sem.at[2])
    gram_ref[...] = summed[...].reshape(256, 128)
    wait_for(packed, PLANE - 1, send_sem.at[0])
    wait_for(along, CHIPS_Z - 1, send_sem.at[1])
    wait_for(summed, PLANE - 1, send_sem.at[2])
    for copy in borders:
        copy.wait_send()


def exchange(cube):
    return pl.pallas_call(
        exchange_kernel,
        out_shape=(
            jax.ShapeDtypeStruct((256, 128), F32),
            jax.ShapeDtypeStruct((HALO, BANDS), BF16),
        ),
        in_specs=[pl.BlockSpec(memory_space=pl.ANY)],
        out_specs=(pl.BlockSpec(memory_space=pltpu.VMEM), pl.BlockSpec(memory_space=pltpu.VMEM)),
        scratch_shapes=[
            pltpu.VMEM((PIXELS, BANDS), BF16),
            pltpu.VMEM((PLANE, 8, 128), F32),
            pltpu.VMEM((PLANE, 8, 128), F32),
            pltpu.VMEM((8, 128), F32),
            pltpu.VMEM((CHIPS_Z, 8, 128), F32),
            pltpu.VMEM((PLANE, 8, 128), F32),
            pltpu.VMEM((SIDE, BANDS), BF16),
            pltpu.VMEM((SIDE, BANDS), BF16),
            pltpu.VMEM((HALO, BANDS), BF16),
            pltpu.SemaphoreType.DMA,
            pltpu.SemaphoreType.DMA((3,)),
            pltpu.SemaphoreType.DMA((3,)),
            pltpu.SemaphoreType.DMA((8,)),
            pltpu.SemaphoreType.DMA((8,)),
        ],
        compiler_params=pltpu.CompilerParams(collective_id=0, has_side_effects=True),
    )(cube)


def split(values):
    high = values.astype(BF16)
    values = values - high.astype(F32)
    middle = values.astype(BF16)
    return high, middle, (values - middle.astype(F32)).astype(BF16)


def unpack(packed):
    row = lax.broadcasted_iota(jnp.int32, (128, 128), 0)
    col = lax.broadcasted_iota(jnp.int32, (128, 128), 1)
    packed = packed * (1.0 / TOTAL_PIXELS)
    mixed, cross = packed[:128], packed[128:]
    flipped = mixed.T
    first = jnp.where(row <= col, mixed, flipped)
    inside = (row < 96) & (col < 96)
    last = jnp.where(inside, jnp.where(row > col, mixed, flipped), 0.0)
    last = jnp.where(inside & (row == col), cross[:, 96:97], last)
    cross = jnp.where(col < 96, cross, 0.0)
    return jnp.concatenate(
        [jnp.concatenate([first, cross], axis=1), jnp.concatenate([cross.T, last], axis=1)], axis=0
    )


def orthonormal(inner, grown):
    row = lax.broadcasted_iota(jnp.int32, (RANK, 128), 0)
    cols = [jnp.broadcast_to(inner[:, k : k + 1], (RANK, 128)) for k in range(RANK)]
    halves = [grown[:, :128], grown[:, 128:]]
    pivots = jnp.zeros((RANK, 128), F32)
    for step in range(RANK):
        pivot = cols[step][step : step + 1]
        pivots = jnp.where(row == step, pivot, pivots)
        if step < RANK - 1:
            factor = jnp.where(row > step, cols[step] * (1.0 / pivot), 0.0)
            for k in range(step + 1, RANK):
                cols[k] = cols[k] - factor * cols[k][step : step + 1]
            halves = [half - factor * half[step : step + 1] for half in halves]
    scale = lax.rsqrt(pivots)
    return jnp.concatenate([half * scale for half in halves], axis=1)


def subspace(packed, start):
    gram = split(unpack(packed))
    basis = start
    for _ in range(POWER_ITERS):
        high, middle, low = split(basis)
        parts = jnp.dot(jnp.concatenate([high, middle, low], axis=0), gram[0], preferred_element_type=F32)
        more = jnp.dot(jnp.concatenate([high, middle], axis=0), gram[1], preferred_element_type=F32)
        least = jnp.dot(high, gram[2], preferred_element_type=F32)
        grown = (
            (parts[2 * RANK :] + more[RANK:] + least)
            + (parts[RANK : 2 * RANK] + more[:RANK])
            + parts[:RANK]
        )
        high, middle, low = split(grown)
        inner = lax.dot_general(
            jnp.concatenate([low, high, middle, middle, high, high], axis=1),
            jnp.concatenate([high, low, middle, high, middle, high], axis=1),
            NT, preferred_element_type=F32,
        )
        basis = orthonormal(inner, grown)
    return basis


def smooth_kernel(
    gram_ref, halo_hbm, cube_hbm, start_ref, out_ref, proj_ref, u0, u1, u2, flow, halo_ref, cube_ref, sems
):
    wide = lax.axis_index("wide")
    narrow = lax.axis_index("narrow")
    load_cube = pltpu.make_async_copy(cube_hbm, cube_ref, sems.at[0])
    load_halo = pltpu.make_async_copy(halo_hbm, halo_ref, sems.at[1])
    load_cube.start()
    load_halo.start()
    basis = subspace(gram_ref[...], start_ref[...])
    low = basis.astype(BF16).astype(F32)
    fit = 4.0 * lax.dot_general(low, basis, TN, precision=HIGHEST, preferred_element_type=F32)
    high, rest, _ = split(fit[:BANDS])
    proj_ref[...] = lax.dot_general(
        basis, basis, TN, precision=HIGHEST, preferred_element_type=F32
    )[:BANDS, :BANDS]

    def fitted(pixels):
        return jnp.dot(pixels, high, preferred_element_type=F32) + jnp.dot(
            pixels, rest, preferred_element_type=F32
        )

    def put(values, rows, row, col, count):
        for half in range(2):
            part = values[:, half * 128 : (half + 1) * 128]
            for r in range(rows):
                u0[half, row + r, col : col + count, :] = part[r * count : (r + 1) * count]

    load_cube.wait()
    load_halo.wait()

    @pl.loop(0, TILE_ROWS // 8)
    def _(index):
        at = pl.multiple_of(index * (8 * TILE_COLS), 8 * TILE_COLS)
        put(fitted(cube_ref[pl.ds(at, 8 * TILE_COLS), :]), 8, DEPTH + index * 8, 8, TILE_COLS)

    borders = fitted(halo_ref[...])
    put(borders[TOP : TOP + BORDER], DEPTH, 0, 8, TILE_COLS)
    put(borders[BOTTOM : BOTTOM + BORDER], DEPTH, DEPTH + TILE_ROWS, 8, TILE_COLS)
    put(borders[LEFT : LEFT + SIDE], TILE_ROWS, DEPTH, 4, 4)
    put(borders[RIGHT : RIGHT + SIDE], TILE_ROWS, DEPTH, 8 + TILE_COLS, 4)
    corners = borders[CORNER:]
    put(corners[4:16], DEPTH, 0, 4, 4)
    put(corners[20:32], DEPTH, 0, 8 + TILE_COLS, 4)
    put(corners[32:44], DEPTH, DEPTH + TILE_ROWS, 4, 4)
    put(corners[48:60], DEPTH, DEPTH + TILE_ROWS, 8 + TILE_COLS, 4)

    stages = (u0, u1, u2)
    for turn in range(TV_ITERS):
        here = stages[turn]
        final = turn == TV_ITERS - 1

        @pl.when(narrow == 0)
        def _():
            here[:, DEPTH - 1] = here[:, DEPTH]

        @pl.when(narrow == N_NARROW - 1)
        def _():
            here[:, DEPTH + TILE_ROWS] = here[:, DEPTH + TILE_ROWS - 1]

        @pl.when(wide == 0)
        def _():
            here[:, :, 7:8, :] = here[:, :, 8:9, :]

        @pl.when(wide == N_WIDE - 1)
        def _():
            here[:, :, 8 + TILE_COLS : 9 + TILE_COLS, :] = here[:, :, 7 + TILE_COLS : 8 + TILE_COLS, :]

        first, count = (8, TILE_COLS) if final else (4, TILE_COLS + 8)

        def flows(half, row, at, size):
            middle = here[half, row, at : at + size, :]
            gx = here[half, row + 1, at : at + size, :] - middle
            gy = here[half, row, at + 1 : at + 1 + size, :] - middle
            scale = lax.rsqrt(gx * gx + gy * gy + 4.0)
            return middle, gx * scale, gy * scale

        def pair(index, above):
            above = list(above)
            for lane in range(2):
                row = turn + 1 + 2 * index + lane
                for half in range(2):
                    middle, px, py = flows(half, row, first, count)
                    flow[lane, half, 8 : 8 + count, :] = py
                    if final:
                        flow[lane, half, 0:8, :] = flows(half, row, 0, 8)[2]
                    change = px - above[half] + (py - flow[lane, half, 7 : 7 + count, :])
                    above[half] = px
                    if turn == 0:
                        value = middle + change
                    else:
                        value = 0.5 * (middle + u0[half, row, first : first + count, :]) + change
                    if final:
                        width = 128 if half == 0 else BANDS - 128
                        at = pl.multiple_of((row - DEPTH) * TILE_COLS, TILE_COLS)
                        out_ref[pl.ds(at, TILE_COLS), half * 128 : half * 128 + width] = (
                            0.25 * value[:, :width]
                        ).astype(BF16)
                    else:
                        stages[turn + 1][half, row, first : first + count, :] = value
            return tuple(above)

        start = tuple(flows(half, turn, first, count)[1] for half in range(2))
        lax.fori_loop(0, (EXT_ROWS - 2 - 2 * turn) // 2, pair, start)


def smooth(gram, halo, cube, start):
    vmem = pl.BlockSpec(memory_space=pltpu.VMEM)
    hbm = pl.BlockSpec(memory_space=pl.ANY)
    field = pltpu.VMEM((2, EXT_ROWS, EXT_COLS + 8, 128), F32)
    return pl.pallas_call(
        smooth_kernel,
        out_shape=(
            jax.ShapeDtypeStruct((PIXELS, BANDS), BF16),
            jax.ShapeDtypeStruct((BANDS, BANDS), F32),
        ),
        in_specs=[vmem, hbm, hbm, vmem],
        out_specs=(vmem, vmem),
        scratch_shapes=[
            field, field, field,
            pltpu.VMEM((2, 2, EXT_COLS + 16, 128), F32),
            pltpu.VMEM((HALO, BANDS), BF16),
            pltpu.VMEM((PIXELS, BANDS), BF16),
            pltpu.SemaphoreType.DMA((2,)),
        ],
    )(gram, halo, cube, start)


def first_basis():
    bands = np.arange(256)[None, :]
    cols = np.arange(RANK)[:, None]
    values = np.cos(np.pi * (bands + 0.5) * cols / BANDS)
    return np.where(bands < BANDS, values, 0.0).astype(np.float32)


def body(cube):
    flat = cube.reshape(PIXELS, BANDS)
    gram, halo = exchange(flat)
    restored, projector = smooth(gram, halo, flat, jnp.asarray(first_basis()))
    return restored.reshape(TILE_ROWS, TILE_COLS, BANDS), projector


def solution(mesh):
    return jax.shard_map(
        body,
        mesh=mesh,
        in_specs=(P("narrow", "wide", None),),
        out_specs=(P("narrow", "wide", None), P()),
        check_vma=False,
    )
```

```python
import functools

import jax
import jax.numpy as jnp
import numpy as np
from jax import lax
from jax.experimental import pallas as pl
from jax.experimental.pallas import tpu as pltpu
from jax.sharding import PartitionSpec as P

TILE_ROWS = 32
TILE_COLS = 48
PIXELS = TILE_ROWS * TILE_COLS
BANDS = 224
RANK = 16
POWER_ITERS = 4
TV_ITERS = 3
CHIPS_X = 4
CHIPS_Z = 8
N_NARROW = 8
N_WIDE = CHIPS_X * CHIPS_Z
PLANE = CHIPS_X * N_NARROW
TOTAL_PIXELS = PIXELS * N_NARROW * N_WIDE
DEPTH = TV_ITERS
BORDER = DEPTH * TILE_COLS
SIDE = TILE_ROWS * 4
TOP, BOTTOM, LEFT, RIGHT, CORNER = 0, BORDER, 2 * BORDER, 2 * BORDER + SIDE, 2 * BORDER + 2 * SIDE
HALO = CORNER + 64
EXT_ROWS = TILE_ROWS + 2 * DEPTH
EXT_COLS = TILE_COLS + 16

PLANE_STEPS = sorted(
    ((dx, dn) for dx in range(CHIPS_X) for dn in range(N_NARROW) if dx or dn),
    key=lambda s: -(2 * min(s[0], CHIPS_X - s[0]) + min(s[1], N_NARROW - s[1])),
)
LINE_STEPS = sorted(range(1, CHIPS_Z), key=lambda s: -min(s, CHIPS_Z - s))

MESH = pl.DeviceIdType.MESH
HIGHEST = lax.Precision.HIGHEST
F32 = jnp.float32
BF16 = jnp.bfloat16
TN = (((0,), (0,)), ((), ()))
NT = (((1,), (1,)), ((), ()))


def select_columns(pixels, first):
    shape = (SIDE, TILE_ROWS * 16)
    want = lax.broadcasted_iota(jnp.int32, shape, 0)
    have = lax.broadcasted_iota(jnp.int32, shape, 1)
    pick = (have == (want // 4) * 16 + want % 4 + first).astype(F32).astype(BF16)
    flat = pixels.reshape(TILE_ROWS * 16, BANDS)
    return jnp.dot(pick, flat, preferred_element_type=F32).astype(BF16)


def exchange_kernel(
    cube_ref, first_ref, gram_ref, halo_ref, tile, start_ref,
    packed, around, own, along, summed, edge_l, edge_r, halo,
    load_sems, send_sem, recv_sem, halo_send, halo_recv,
):
    wide = lax.axis_index("wide")
    narrow = lax.axis_index("narrow")
    z = wide // CHIPS_X
    x = wide % CHIPS_X
    block = x * N_NARROW + narrow

    load = pltpu.make_async_copy(cube_ref, tile, load_sems.at[0])
    load.start()
    load_first = pltpu.make_async_copy(first_ref, start_ref, load_sems.at[1])
    load_first.start()

    def in_plane(dx, dn):
        other_x, other_n = (x + dx) % CHIPS_X, (narrow + dn) % N_NARROW
        return (z * CHIPS_X + other_x, other_n), other_x * N_NARROW + other_n

    def on_line(step):
        return (((z + step) % CHIPS_Z) * CHIPS_X + x, narrow)

    def beside(dr, dc):
        return ((wide + dc + N_WIDE) % N_WIDE, (narrow + dr + N_NARROW) % N_NARROW)

    barrier = pltpu.get_barrier_semaphore()

    for dx, dn in PLANE_STEPS:
        pl.semaphore_signal(barrier, inc=1, device_id=in_plane(dx, dn)[0], device_id_type=MESH)
    for step in LINE_STEPS:
        pl.semaphore_signal(barrier, inc=1, device_id=on_line(step), device_id_type=MESH)
    for dr in (-1, 0, 1):
        for dc in (-1, 0, 1):
            if dr or dc:
                pl.semaphore_signal(barrier, inc=1, device_id=beside(dr, dc), device_id_type=MESH)

    load.wait()
    load_first.wait()
    values = tile[...]
    local = lax.dot_general(values, values, TN, preferred_element_type=F32)
    row = lax.broadcasted_iota(jnp.int32, (128, 128), 0)
    col = lax.broadcasted_iota(jnp.int32, (128, 128), 1)
    first = local[:128, :128]
    cross = jnp.concatenate([local[:128, 128:], jnp.zeros((128, 32), F32)], axis=1)
    last = jnp.concatenate([local[128:, 128:], jnp.zeros((96, 32), F32)], axis=1)
    last = jnp.concatenate([last, jnp.zeros((32, 128), F32)], axis=0)
    diagonal = jnp.sum(jnp.where(row == col, last, 0.0), axis=1, keepdims=True)
    packed[:16] = jnp.where(row <= col, first, last).reshape(16, 8, 128)
    packed[16:] = jnp.where(col == 96, diagonal, cross).reshape(16, 8, 128)

    pl.semaphore_wait(barrier, PLANE - 1 + CHIPS_Z - 1 + 8)

    for slot, (dx, dn) in enumerate(PLANE_STEPS):
        device, other = in_plane(dx, dn)
        pltpu.make_async_remote_copy(
            src_ref=packed.at[other], dst_ref=around.at[slot],
            send_sem=send_sem.at[0], recv_sem=recv_sem.at[0],
            device_id=device, device_id_type=MESH,
        ).start()

    grid = values.reshape(TILE_ROWS, TILE_COLS, BANDS)
    edge_l[...] = select_columns(grid[:, :16], 0)
    edge_r[...] = select_columns(grid[:, 32:], 12)

    def wait_for(ref, count, sem):
        part = ref.at[pl.ds(0, count)]
        pltpu.make_async_copy(part, part, sem).wait()

    wait_for(around, PLANE - 1, recv_sem.at[0])
    total = packed[block]
    for step in range(PLANE - 1):
        total = total + around[step]
    own[...] = total
    along[z] = total

    for step in LINE_STEPS:
        pltpu.make_async_remote_copy(
            src_ref=own, dst_ref=along.at[z],
            send_sem=send_sem.at[1], recv_sem=recv_sem.at[1],
            device_id=on_line(step), device_id_type=MESH,
        ).start()

    pieces = (
        (-1, 0, tile.at[pl.ds(0, BORDER)], BOTTOM, BORDER),
        (1, 0, tile.at[pl.ds(PIXELS - BORDER, BORDER)], TOP, BORDER),
        (0, -1, edge_l, RIGHT, SIDE),
        (0, 1, edge_r, LEFT, SIDE),
        (-1, -1, edge_l.at[pl.ds(0, 16)], CORNER + 48, 16),
        (1, -1, edge_l.at[pl.ds(SIDE - 16, 16)], CORNER + 16, 16),
        (-1, 1, edge_r.at[pl.ds(0, 16)], CORNER + 32, 16),
        (1, 1, edge_r.at[pl.ds(SIDE - 16, 16)], CORNER, 16),
    )
    borders = []
    for index, (dr, dc, source, at, size) in enumerate(pieces):
        copy = pltpu.make_async_remote_copy(
            src_ref=source, dst_ref=halo.at[pl.ds(at, size)],
            send_sem=halo_send.at[index], recv_sem=halo_recv.at[index],
            device_id=beside(dr, dc), device_id_type=MESH,
        )
        copy.start()
        borders.append(copy)

    wait_for(along, CHIPS_Z - 1, recv_sem.at[1])
    total = along[0]
    for step in range(1, CHIPS_Z):
        total = total + along[step]
    summed[block] = total

    for dx, dn in PLANE_STEPS:
        pltpu.make_async_remote_copy(
            src_ref=summed.at[block], dst_ref=summed.at[block],
            send_sem=send_sem.at[2], recv_sem=recv_sem.at[2],
            device_id=in_plane(dx, dn)[0], device_id_type=MESH,
        ).start()

    for copy in borders:
        copy.wait_recv()
    halo_ref[...] = halo[...]
    wait_for(summed, PLANE - 1, recv_sem.at[2])
    gram_ref[...] = summed[...].reshape(256, 128)
    wait_for(packed, PLANE - 1, send_sem.at[0])
    wait_for(along, CHIPS_Z - 1, send_sem.at[1])
    wait_for(summed, PLANE - 1, send_sem.at[2])
    for copy in borders:
        copy.wait_send()


def exchange(cube, first):
    vmem = pl.BlockSpec(memory_space=pltpu.VMEM)
    hbm = pl.BlockSpec(memory_space=pltpu.HBM)
    return pl.pallas_call(
        exchange_kernel,
        out_shape=(
            jax.ShapeDtypeStruct((256, 128), F32),
            jax.ShapeDtypeStruct((HALO, BANDS), BF16),
            jax.ShapeDtypeStruct((PIXELS, BANDS), BF16),
            jax.ShapeDtypeStruct((RANK, 256), F32),
        ),
        in_specs=[hbm, hbm],
        out_specs=(vmem, vmem, vmem, vmem),
        scratch_shapes=[
            pltpu.VMEM((PLANE, 8, 128), F32),
            pltpu.VMEM((PLANE, 8, 128), F32),
            pltpu.VMEM((8, 128), F32),
            pltpu.VMEM((CHIPS_Z, 8, 128), F32),
            pltpu.VMEM((PLANE, 8, 128), F32),
            pltpu.VMEM((SIDE, BANDS), BF16),
            pltpu.VMEM((SIDE, BANDS), BF16),
            pltpu.VMEM((HALO, BANDS), BF16),
            pltpu.SemaphoreType.DMA((2,)),
            pltpu.SemaphoreType.DMA((3,)),
            pltpu.SemaphoreType.DMA((3,)),
            pltpu.SemaphoreType.DMA((8,)),
            pltpu.SemaphoreType.DMA((8,)),
        ],
        compiler_params=pltpu.CompilerParams(collective_id=0, has_side_effects=True, vmem_limit_bytes=12 << 20),
    )(cube, first)


def split(values):
    high = values.astype(BF16)
    values = values - high.astype(F32)
    middle = values.astype(BF16)
    return high, middle, (values - middle.astype(F32)).astype(BF16)


def unpack(packed):
    row = lax.broadcasted_iota(jnp.int32, (128, 128), 0)
    col = lax.broadcasted_iota(jnp.int32, (128, 128), 1)
    packed = packed * (1.0 / TOTAL_PIXELS)
    mixed, cross = packed[:128], packed[128:]
    flipped = mixed.T
    first = jnp.where(row <= col, mixed, flipped)
    inside = (row < 96) & (col < 96)
    last = jnp.where(inside, jnp.where(row > col, mixed, flipped), 0.0)
    last = jnp.where(inside & (row == col), cross[:, 96:97], last)
    cross = jnp.where(col < 96, cross, 0.0)
    return jnp.concatenate(
        [jnp.concatenate([first, cross], axis=1), jnp.concatenate([cross.T, last], axis=1)], axis=0
    )


def orthonormal(inner, grown):
    row = lax.broadcasted_iota(jnp.int32, (RANK, 128), 0)
    cols = [jnp.broadcast_to(inner[:, k : k + 1], (RANK, 128)) for k in range(RANK)]
    halves = [grown[:, :128], grown[:, 128:]]
    pivots = jnp.zeros((RANK, 128), F32)
    for step in range(RANK):
        pivot = cols[step][step : step + 1]
        pivots = jnp.where(row == step, pivot, pivots)
        if step < RANK - 1:
            factor = jnp.where(row > step, cols[step] * (1.0 / pivot), 0.0)
            for k in range(step + 1, RANK):
                cols[k] = cols[k] - factor * cols[k][step : step + 1]
            halves = [half - factor * half[step : step + 1] for half in halves]
    scale = lax.rsqrt(pivots)
    return jnp.concatenate([half * scale for half in halves], axis=1)


def subspace(packed, start):
    gram = split(unpack(packed))
    basis = start
    for _ in range(POWER_ITERS):
        high, middle, low = split(basis)
        parts = jnp.dot(jnp.concatenate([high, middle, low], axis=0), gram[0], preferred_element_type=F32)
        more = jnp.dot(jnp.concatenate([high, middle], axis=0), gram[1], preferred_element_type=F32)
        least = jnp.dot(high, gram[2], preferred_element_type=F32)
        grown = (
            (parts[2 * RANK :] + more[RANK:] + least)
            + (parts[RANK : 2 * RANK] + more[:RANK])
            + parts[:RANK]
        )
        high, middle, low = split(grown)
        inner = lax.dot_general(
            jnp.concatenate([low, high, middle, middle, high, high], axis=1),
            jnp.concatenate([high, low, middle, high, middle, high], axis=1),
            NT, preferred_element_type=F32,
        )
        basis = orthonormal(inner, grown)
    return basis


def smooth_kernel(
    gram_ref, halo_ref, cube_ref, start_ref, out_hbm, proj_hbm, u0, u1, u2, flow, out_ref, proj_ref, sems
):
    wide = lax.axis_index("wide")
    narrow = lax.axis_index("narrow")
    basis = subspace(gram_ref[...], start_ref[...])
    low = basis.astype(BF16).astype(F32)
    fit = 4.0 * lax.dot_general(low, basis, TN, precision=HIGHEST, preferred_element_type=F32)
    high, rest, _ = split(fit[:BANDS])
    proj_ref[...] = lax.dot_general(
        basis, basis, TN, precision=HIGHEST, preferred_element_type=F32
    )[:BANDS, :BANDS]

    def fitted(pixels):
        return jnp.dot(pixels, high, preferred_element_type=F32) + jnp.dot(
            pixels, rest, preferred_element_type=F32
        )

    def put(values, rows, row, col, count):
        for half in range(2):
            part = values[:, half * 128 : (half + 1) * 128]
            for r in range(rows):
                u0[half, row + r, col : col + count, :] = part[r * count : (r + 1) * count]

    proj_copy = pltpu.make_async_copy(proj_ref, proj_hbm, sems.at[4])
    proj_copy.start()

    @pl.loop(0, TILE_ROWS // 8)
    def _(index):
        at = pl.multiple_of(index * (8 * TILE_COLS), 8 * TILE_COLS)
        put(fitted(cube_ref[pl.ds(at, 8 * TILE_COLS), :]), 8, DEPTH + index * 8, 8, TILE_COLS)

    borders = fitted(halo_ref[...])
    put(borders[TOP : TOP + BORDER], DEPTH, 0, 8, TILE_COLS)
    put(borders[BOTTOM : BOTTOM + BORDER], DEPTH, DEPTH + TILE_ROWS, 8, TILE_COLS)
    put(borders[LEFT : LEFT + SIDE], TILE_ROWS, DEPTH, 4, 4)
    put(borders[RIGHT : RIGHT + SIDE], TILE_ROWS, DEPTH, 8 + TILE_COLS, 4)
    corners = borders[CORNER:]
    put(corners[4:16], DEPTH, 0, 4, 4)
    put(corners[20:32], DEPTH, 0, 8 + TILE_COLS, 4)
    put(corners[32:44], DEPTH, DEPTH + TILE_ROWS, 4, 4)
    put(corners[48:60], DEPTH, DEPTH + TILE_ROWS, 8 + TILE_COLS, 4)

    stages = (u0, u1, u2)
    for turn in range(TV_ITERS):
        here = stages[turn]
        final = turn == TV_ITERS - 1

        @pl.when(narrow == 0)
        def _():
            here[:, DEPTH - 1] = here[:, DEPTH]

        @pl.when(narrow == N_NARROW - 1)
        def _():
            here[:, DEPTH + TILE_ROWS] = here[:, DEPTH + TILE_ROWS - 1]

        @pl.when(wide == 0)
        def _():
            here[:, :, 7:8, :] = here[:, :, 8:9, :]

        @pl.when(wide == N_WIDE - 1)
        def _():
            here[:, :, 8 + TILE_COLS : 9 + TILE_COLS, :] = here[:, :, 7 + TILE_COLS : 8 + TILE_COLS, :]

        first, count = (8, TILE_COLS) if final else (4, TILE_COLS + 8)

        def flows(half, row, at, size):
            middle = here[half, row, at : at + size, :]
            gx = here[half, row + 1, at : at + size, :] - middle
            gy = here[half, row, at + 1 : at + 1 + size, :] - middle
            scale = lax.rsqrt(gx * gx + gy * gy + 4.0)
            return middle, gx * scale, gy * scale

        def pair(index, above):
            above = list(above)
            for lane in range(2):
                row = turn + 1 + 2 * index + lane
                for half in range(2):
                    middle, px, py = flows(half, row, first, count)
                    flow[lane, half, 8 : 8 + count, :] = py
                    if final:
                        flow[lane, half, 0:8, :] = flows(half, row, 0, 8)[2]
                    change = px - above[half] + (py - flow[lane, half, 7 : 7 + count, :])
                    above[half] = px
                    if turn == 0:
                        value = middle + change
                    else:
                        value = 0.5 * (middle + u0[half, row, first : first + count, :]) + change
                    if final:
                        width = 128 if half == 0 else BANDS - 128
                        at = pl.multiple_of((row - DEPTH) * TILE_COLS, TILE_COLS)
                        out_ref[pl.ds(at, TILE_COLS), half * 128 : half * 128 + width] = (
                            0.25 * value[:, :width]
                        ).astype(BF16)
                    else:
                        stages[turn + 1][half, row, first : first + count, :] = value
            return tuple(above)

        above = tuple(flows(half, turn, first, count)[1] for half in range(2))
        if not final:
            lax.fori_loop(0, (EXT_ROWS - 2 - 2 * turn) // 2, pair, above)
            continue
        copies = []
        for part in range(4):
            above = lax.fori_loop(part * 4, part * 4 + 4, pair, above)
            rows = pl.ds(part * (PIXELS // 4), PIXELS // 4)
            copy = pltpu.make_async_copy(out_ref.at[rows], out_hbm.at[rows], sems.at[part])
            copy.start()
            copies.append(copy)
        for copy in copies + [proj_copy]:
            copy.wait()


def smooth(gram, halo, cube, start):
    vmem = pl.BlockSpec(memory_space=pltpu.VMEM)
    hbm = pl.BlockSpec(memory_space=pltpu.HBM)
    field = pltpu.VMEM((2, EXT_ROWS, EXT_COLS + 8, 128), F32)
    return pl.pallas_call(
        smooth_kernel,
        out_shape=(
            jax.ShapeDtypeStruct((PIXELS, BANDS), BF16),
            jax.ShapeDtypeStruct((BANDS, BANDS), F32),
        ),
        in_specs=[vmem] * 4,
        out_specs=(hbm, hbm),
        scratch_shapes=[
            field, field, field,
            pltpu.VMEM((2, 2, EXT_COLS + 16, 128), F32),
            pltpu.VMEM((PIXELS, BANDS), BF16),
            pltpu.VMEM((BANDS, BANDS), F32),
            pltpu.SemaphoreType.DMA((5,)),
        ],
        compiler_params=pltpu.CompilerParams(vmem_limit_bytes=24 << 20),
    )(gram, halo, cube, start)


def first_basis():
    bands = np.arange(256)[None, :]
    cols = np.arange(RANK)[:, None]
    values = np.cos(np.pi * (bands + 0.5) * cols / BANDS)
    return np.where(bands < BANDS, values, 0.0).astype(np.float32)


def body(cube):
    flat = cube.reshape(PIXELS, BANDS)
    flat = pltpu.with_memory_space_constraint(flat, pltpu.HBM)
    first = pltpu.with_memory_space_constraint(jnp.asarray(first_basis()), pltpu.HBM)
    restored, projector = smooth(*exchange(flat, first))
    return restored.reshape(TILE_ROWS, TILE_COLS, BANDS), projector


def solution(mesh):
    return jax.shard_map(
        body,
        mesh=mesh,
        in_specs=(P("narrow", "wide", None),),
        out_specs=(P("narrow", "wide", None), P()),
        check_vma=False,
    )
```

```python
import functools

import jax
import jax.numpy as jnp
import numpy as np
from jax import lax
from jax.experimental import pallas as pl
from jax.experimental.pallas import tpu as pltpu
from jax.sharding import PartitionSpec as P

TILE_ROWS = 32
TILE_COLS = 48
PIXELS = TILE_ROWS * TILE_COLS
BANDS = 224
RANK = 16
POWER_ITERS = 4
TV_ITERS = 3
CHIPS_X = 4
CHIPS_Z = 8
N_NARROW = 8
N_WIDE = CHIPS_X * CHIPS_Z
PLANE = CHIPS_X * N_NARROW
TOTAL_PIXELS = PIXELS * N_NARROW * N_WIDE
DEPTH = TV_ITERS
BORDER = DEPTH * TILE_COLS
SIDE = TILE_ROWS * 4
TOP, BOTTOM, LEFT, RIGHT, CORNER = 0, BORDER, 2 * BORDER, 2 * BORDER + SIDE, 2 * BORDER + 2 * SIDE
HALO = CORNER + 64
EXT_ROWS = TILE_ROWS + 2 * DEPTH
EXT_COLS = TILE_COLS + 16

PLANE_STEPS = sorted(
    ((dx, dn) for dx in range(CHIPS_X) for dn in range(N_NARROW) if dx or dn),
    key=lambda s: -(2 * min(s[0], CHIPS_X - s[0]) + min(s[1], N_NARROW - s[1])),
)
LINE_STEPS = sorted(range(1, CHIPS_Z), key=lambda s: -min(s, CHIPS_Z - s))

MESH = pl.DeviceIdType.MESH
HIGHEST = lax.Precision.HIGHEST
F32 = jnp.float32
BF16 = jnp.bfloat16
TN = (((0,), (0,)), ((), ()))
NT = (((1,), (1,)), ((), ()))


def select_columns(pixels, first):
    shape = (SIDE, TILE_ROWS * 16)
    want = lax.broadcasted_iota(jnp.int32, shape, 0)
    have = lax.broadcasted_iota(jnp.int32, shape, 1)
    pick = (have == (want // 4) * 16 + want % 4 + first).astype(F32).astype(BF16)
    flat = pixels.reshape(TILE_ROWS * 16, BANDS)
    return jnp.dot(pick, flat, preferred_element_type=F32).astype(BF16)


def exchange_kernel(
    cube_ref, first_ref, gram_ref, halo_ref, tile, start_ref,
    packed, around, own, along, summed, edge_l, edge_r, halo,
    load_sems, send_sem, recv_sem, halo_send, halo_recv,
):
    wide = lax.axis_index("wide")
    narrow = lax.axis_index("narrow")
    z = wide // CHIPS_X
    x = wide % CHIPS_X
    block = x * N_NARROW + narrow

    load = pltpu.make_async_copy(cube_ref, tile, load_sems.at[0])
    load.start()
    load_first = pltpu.make_async_copy(first_ref, start_ref, load_sems.at[1])
    load_first.start()

    def in_plane(dx, dn):
        other_x, other_n = (x + dx) % CHIPS_X, (narrow + dn) % N_NARROW
        return (z * CHIPS_X + other_x, other_n), other_x * N_NARROW + other_n

    def on_line(step):
        return (((z + step) % CHIPS_Z) * CHIPS_X + x, narrow)

    def beside(dr, dc):
        return ((wide + dc + N_WIDE) % N_WIDE, (narrow + dr + N_NARROW) % N_NARROW)

    barrier = pltpu.get_barrier_semaphore()

    for dx, dn in PLANE_STEPS:
        pl.semaphore_signal(barrier, inc=1, device_id=in_plane(dx, dn)[0], device_id_type=MESH)
    for step in LINE_STEPS:
        pl.semaphore_signal(barrier, inc=1, device_id=on_line(step), device_id_type=MESH)
    for dr in (-1, 0, 1):
        for dc in (-1, 0, 1):
            if dr or dc:
                pl.semaphore_signal(barrier, inc=1, device_id=beside(dr, dc), device_id_type=MESH)

    load.wait()
    load_first.wait()
    values = tile[...]
    local = lax.dot_general(values, values, TN, preferred_element_type=F32)
    row = lax.broadcasted_iota(jnp.int32, (128, 128), 0)
    col = lax.broadcasted_iota(jnp.int32, (128, 128), 1)
    first = local[:128, :128]
    cross = jnp.concatenate([local[:128, 128:], jnp.zeros((128, 32), F32)], axis=1)
    last = jnp.concatenate([local[128:, 128:], jnp.zeros((96, 32), F32)], axis=1)
    last = jnp.concatenate([last, jnp.zeros((32, 128), F32)], axis=0)
    diagonal = jnp.sum(jnp.where(row == col, last, 0.0), axis=1, keepdims=True)
    packed[:16] = jnp.where(row <= col, first, last).reshape(16, 8, 128)
    packed[16:] = jnp.where(col == 96, diagonal, cross).reshape(16, 8, 128)

    pl.semaphore_wait(barrier, PLANE - 1 + CHIPS_Z - 1 + 8)

    for slot, (dx, dn) in enumerate(PLANE_STEPS):
        device, other = in_plane(dx, dn)
        pltpu.make_async_remote_copy(
            src_ref=packed.at[other], dst_ref=around.at[slot],
            send_sem=send_sem.at[0], recv_sem=recv_sem.at[0],
            device_id=device, device_id_type=MESH,
        ).start()

    grid = values.reshape(TILE_ROWS, TILE_COLS, BANDS)
    edge_l[...] = select_columns(grid[:, :16], 0)
    edge_r[...] = select_columns(grid[:, 32:], 12)

    def wait_for(ref, count, sem):
        part = ref.at[pl.ds(0, count)]
        pltpu.make_async_copy(part, part, sem).wait()

    wait_for(around, PLANE - 1, recv_sem.at[0])
    total = packed[block]
    for step in range(PLANE - 1):
        total = total + around[step]
    own[...] = total
    along[z] = total

    for step in LINE_STEPS:
        pltpu.make_async_remote_copy(
            src_ref=own, dst_ref=along.at[z],
            send_sem=send_sem.at[1], recv_sem=recv_sem.at[1],
            device_id=on_line(step), device_id_type=MESH,
        ).start()

    pieces = (
        (-1, 0, tile.at[pl.ds(0, BORDER)], BOTTOM, BORDER),
        (1, 0, tile.at[pl.ds(PIXELS - BORDER, BORDER)], TOP, BORDER),
        (0, -1, edge_l, RIGHT, SIDE),
        (0, 1, edge_r, LEFT, SIDE),
        (-1, -1, edge_l.at[pl.ds(0, 16)], CORNER + 48, 16),
        (1, -1, edge_l.at[pl.ds(SIDE - 16, 16)], CORNER + 16, 16),
        (-1, 1, edge_r.at[pl.ds(0, 16)], CORNER + 32, 16),
        (1, 1, edge_r.at[pl.ds(SIDE - 16, 16)], CORNER, 16),
    )
    borders = []
    for index, (dr, dc, source, at, size) in enumerate(pieces):
        copy = pltpu.make_async_remote_copy(
            src_ref=source, dst_ref=halo.at[pl.ds(at, size)],
            send_sem=halo_send.at[index], recv_sem=halo_recv.at[index],
            device_id=beside(dr, dc), device_id_type=MESH,
        )
        copy.start()
        borders.append(copy)

    wait_for(along, CHIPS_Z - 1, recv_sem.at[1])
    total = along[0]
    for step in range(1, CHIPS_Z):
        total = total + along[step]
    summed[block] = total

    for dx, dn in PLANE_STEPS:
        pltpu.make_async_remote_copy(
            src_ref=summed.at[block], dst_ref=summed.at[block],
            send_sem=send_sem.at[2], recv_sem=recv_sem.at[2],
            device_id=in_plane(dx, dn)[0], device_id_type=MESH,
        ).start()

    for copy in borders:
        copy.wait_recv()
    halo_ref[...] = halo[...]
    wait_for(summed, PLANE - 1, recv_sem.at[2])
    gram_ref[...] = summed[...].reshape(256, 128)
    wait_for(packed, PLANE - 1, send_sem.at[0])
    wait_for(along, CHIPS_Z - 1, send_sem.at[1])
    wait_for(summed, PLANE - 1, send_sem.at[2])
    for copy in borders:
        copy.wait_send()


def exchange(cube, first):
    vmem = pl.BlockSpec(memory_space=pltpu.VMEM)
    hbm = pl.BlockSpec(memory_space=pltpu.HBM)
    return pl.pallas_call(
        exchange_kernel,
        out_shape=(
            jax.ShapeDtypeStruct((256, 128), F32),
            jax.ShapeDtypeStruct((HALO, BANDS), BF16),
            jax.ShapeDtypeStruct((PIXELS, BANDS), BF16),
            jax.ShapeDtypeStruct((RANK, 256), F32),
        ),
        in_specs=[hbm, hbm],
        out_specs=(vmem, vmem, vmem, vmem),
        scratch_shapes=[
            pltpu.VMEM((PLANE, 8, 128), F32),
            pltpu.VMEM((PLANE, 8, 128), F32),
            pltpu.VMEM((8, 128), F32),
            pltpu.VMEM((CHIPS_Z, 8, 128), F32),
            pltpu.VMEM((PLANE, 8, 128), F32),
            pltpu.VMEM((SIDE, BANDS), BF16),
            pltpu.VMEM((SIDE, BANDS), BF16),
            pltpu.VMEM((HALO, BANDS), BF16),
            pltpu.SemaphoreType.DMA((2,)),
            pltpu.SemaphoreType.DMA((3,)),
            pltpu.SemaphoreType.DMA((3,)),
            pltpu.SemaphoreType.DMA((8,)),
            pltpu.SemaphoreType.DMA((8,)),
        ],
        compiler_params=pltpu.CompilerParams(collective_id=0, has_side_effects=True, vmem_limit_bytes=12 << 20),
    )(cube, first)


def split(values):
    high = values.astype(BF16)
    values = values - high.astype(F32)
    middle = values.astype(BF16)
    return high, middle, (values - middle.astype(F32)).astype(BF16)


def unpack(packed):
    row = lax.broadcasted_iota(jnp.int32, (128, 128), 0)
    col = lax.broadcasted_iota(jnp.int32, (128, 128), 1)
    packed = packed * (1.0 / TOTAL_PIXELS)
    mixed, cross = packed[:128], packed[128:]
    flipped = mixed.T
    first = jnp.where(row <= col, mixed, flipped)
    inside = (row < 96) & (col < 96)
    last = jnp.where(inside, jnp.where(row > col, mixed, flipped), 0.0)
    last = jnp.where(inside & (row == col), cross[:, 96:97], last)
    cross = jnp.where(col < 96, cross, 0.0)
    return jnp.concatenate(
        [jnp.concatenate([first, cross], axis=1), jnp.concatenate([cross.T, last], axis=1)], axis=0
    )


def orthonormal(inner, grown):
    row = lax.broadcasted_iota(jnp.int32, (8, 128), 0)

    def spread(k, half):
        return jnp.broadcast_to(inner[8 * half : 8 * half + 8, k : k + 1], (8, 128))

    cols = [[spread(k, 0) if k < 8 else None, spread(k, 1)] for k in range(RANK)]
    rows = [[grown[8 * half : 8 * half + 8, at : at + 128] for at in (0, 128)] for half in range(2)]
    pivots = [jnp.zeros((8, 128), F32)] * 2
    for step in range(RANK):
        own, local = step // 8, step % 8
        column = cols[step]
        pivot = column[own][local : local + 1]
        pivots[own] = jnp.where(row == local, pivot, pivots[own])
        if step == RANK - 1:
            break
        inverse = 1.0 / pivot
        factor = [None, None]
        for half in range(own, 2):
            factor[half] = column[half] * inverse
        factor[own] = jnp.where(row > local, factor[own], 0.0)
        for k in range(step + 1, RANK):
            value = column[k // 8][k % 8 : k % 8 + 1]
            for half in range(k // 8, 2):
                cols[k][half] = cols[k][half] - factor[half] * value
        lead = [values[local : local + 1] for values in rows[own]]
        for half in range(own, 2):
            rows[half] = [values - factor[half] * top for values, top in zip(rows[half], lead)]
    scaled = [[values * lax.rsqrt(pivots[half]) for values in rows[half]] for half in range(2)]
    return jnp.concatenate([jnp.concatenate(part, axis=1) for part in scaled], axis=0)


def subspace(packed, start):
    gram = split(unpack(packed))
    basis = start
    for _ in range(POWER_ITERS):
        high, middle, low = split(basis)
        parts = jnp.dot(jnp.concatenate([high, middle, low], axis=0), gram[0], preferred_element_type=F32)
        more = jnp.dot(jnp.concatenate([high, middle], axis=0), gram[1], preferred_element_type=F32)
        least = jnp.dot(high, gram[2], preferred_element_type=F32)
        grown = (
            (parts[2 * RANK :] + more[RANK:] + least)
            + (parts[RANK : 2 * RANK] + more[:RANK])
            + parts[:RANK]
        )
        high, middle, low = split(grown)
        inner = lax.dot_general(
            jnp.concatenate([low, high, middle, middle, high, high], axis=1),
            jnp.concatenate([high, low, middle, high, middle, high], axis=1),
            NT, preferred_element_type=F32,
        )
        basis = orthonormal(inner, grown)
    return basis


def smooth_kernel(
    gram_ref, halo_ref, cube_ref, start_ref, out_hbm, proj_hbm, u0, u1, u2, flow, out_ref, proj_ref, sems
):
    wide = lax.axis_index("wide")
    narrow = lax.axis_index("narrow")
    basis = subspace(gram_ref[...], start_ref[...])
    first, second, third = split(basis)

    def outer(left, right):
        return lax.dot_general(
            jnp.concatenate(left, axis=0), jnp.concatenate(right, axis=0), TN, preferred_element_type=F32
        )

    fit = outer([first] * 3, [third, second, first])
    high, rest, _ = split(4.0 * fit[:BANDS])
    proj_ref[...] = (fit + outer([third, second, second], [first, second, first]))[:BANDS, :BANDS]

    def fitted(pixels):
        return jnp.dot(pixels, high, preferred_element_type=F32) + jnp.dot(
            pixels, rest, preferred_element_type=F32
        )

    def put(values, rows, row, col, count):
        for half in range(2):
            part = values[:, half * 128 : (half + 1) * 128]
            for r in range(rows):
                u0[half, row + r, col : col + count, :] = part[r * count : (r + 1) * count]

    proj_copy = pltpu.make_async_copy(proj_ref, proj_hbm, sems.at[4])
    proj_copy.start()

    put(fitted(cube_ref[...]), TILE_ROWS, DEPTH, 8, TILE_COLS)
    borders = fitted(halo_ref[...])
    put(borders[TOP : TOP + BORDER], DEPTH, 0, 8, TILE_COLS)
    put(borders[BOTTOM : BOTTOM + BORDER], DEPTH, DEPTH + TILE_ROWS, 8, TILE_COLS)
    put(borders[LEFT : LEFT + SIDE], TILE_ROWS, DEPTH, 4, 4)
    put(borders[RIGHT : RIGHT + SIDE], TILE_ROWS, DEPTH, 8 + TILE_COLS, 4)
    corners = borders[CORNER:]
    put(corners[4:16], DEPTH, 0, 4, 4)
    put(corners[20:32], DEPTH, 0, 8 + TILE_COLS, 4)
    put(corners[32:44], DEPTH, DEPTH + TILE_ROWS, 4, 4)
    put(corners[48:60], DEPTH, DEPTH + TILE_ROWS, 8 + TILE_COLS, 4)

    stages = (u0, u1, u2)
    for turn in range(TV_ITERS):
        here = stages[turn]
        final = turn == TV_ITERS - 1

        @pl.when(narrow == 0)
        def _():
            here[:, DEPTH - 1] = here[:, DEPTH]

        @pl.when(narrow == N_NARROW - 1)
        def _():
            here[:, DEPTH + TILE_ROWS] = here[:, DEPTH + TILE_ROWS - 1]

        @pl.when(wide == 0)
        def _():
            here[:, :, 7:8, :] = here[:, :, 8:9, :]

        @pl.when(wide == N_WIDE - 1)
        def _():
            here[:, :, 8 + TILE_COLS : 9 + TILE_COLS, :] = here[:, :, 7 + TILE_COLS : 8 + TILE_COLS, :]

        first, count = (8, TILE_COLS) if final else (4, TILE_COLS + 8)

        def flows(half, row, at, size):
            middle = here[half, row, at : at + size, :]
            gx = here[half, row + 1, at : at + size, :] - middle
            gy = here[half, row, at + 1 : at + 1 + size, :] - middle
            scale = lax.rsqrt(gx * gx + gy * gy + 4.0)
            return middle, gx * scale, gy * scale

        unroll = (4, 4, 4)[turn]

        def lines(index, above, count_rows, base):
            above = list(above)
            for lane in range(count_rows):
                row = base + count_rows * index + lane
                for half in range(2):
                    middle, px, py = flows(half, row, first, count)
                    flow[lane, half, 8 : 8 + count, :] = py
                    if final:
                        flow[lane, half, 0:8, :] = flows(half, row, 0, 8)[2]
                    change = px - above[half] + (py - flow[lane, half, 7 : 7 + count, :])
                    above[half] = px
                    if turn == 0:
                        value = middle + change
                    else:
                        value = 0.5 * (middle + u0[half, row, first : first + count, :]) + change
                    if final:
                        width = 128 if half == 0 else BANDS - 128
                        at = pl.multiple_of((row - DEPTH) * TILE_COLS, TILE_COLS)
                        out_ref[pl.ds(at, TILE_COLS), half * 128 : half * 128 + width] = (
                            0.25 * value[:, :width]
                        ).astype(BF16)
                    else:
                        stages[turn + 1][half, row, first : first + count, :] = value
            return tuple(above)

        above = tuple(flows(half, turn, first, count)[1] for half in range(2))
        if not final:
            rows = EXT_ROWS - 2 - 2 * turn
            steps = rows // unroll
            above = lax.fori_loop(0, steps, lambda i, c: lines(i, c, unroll, turn + 1), above)
            if rows % unroll:
                lines(0, above, rows % unroll, turn + 1 + steps * unroll)
            continue
        copies = []
        for part in range(4):
            base = DEPTH + 8 * part
            above = lax.fori_loop(0, 8 // unroll, lambda i, c, base=base: lines(i, c, unroll, base), above)
            rows = pl.ds(part * (PIXELS // 4), PIXELS // 4)
            copy = pltpu.make_async_copy(out_ref.at[rows], out_hbm.at[rows], sems.at[part])
            copy.start()
            copies.append(copy)
        for copy in copies + [proj_copy]:
            copy.wait()


def smooth(gram, halo, cube, start):
    vmem = pl.BlockSpec(memory_space=pltpu.VMEM)
    hbm = pl.BlockSpec(memory_space=pltpu.HBM)
    field = pltpu.VMEM((2, EXT_ROWS, EXT_COLS + 8, 128), F32)
    return pl.pallas_call(
        smooth_kernel,
        out_shape=(
            jax.ShapeDtypeStruct((PIXELS, BANDS), BF16),
            jax.ShapeDtypeStruct((BANDS, BANDS), F32),
        ),
        in_specs=[vmem] * 4,
        out_specs=(hbm, hbm),
        scratch_shapes=[
            field, field, field,
            pltpu.VMEM((8, 2, EXT_COLS + 16, 128), F32),
            pltpu.VMEM((PIXELS, BANDS), BF16),
            pltpu.VMEM((BANDS, BANDS), F32),
            pltpu.SemaphoreType.DMA((5,)),
        ],
        compiler_params=pltpu.CompilerParams(vmem_limit_bytes=24 << 20),
    )(gram, halo, cube, start)


def first_basis():
    bands = np.arange(256)[None, :]
    cols = np.arange(RANK)[:, None]
    values = np.cos(np.pi * (bands + 0.5) * cols / BANDS)
    return np.where(bands < BANDS, values, 0.0).astype(np.float32)


def body(cube):
    flat = cube.reshape(PIXELS, BANDS)
    flat = pltpu.with_memory_space_constraint(flat, pltpu.HBM)
    first = pltpu.with_memory_space_constraint(jnp.asarray(first_basis()), pltpu.HBM)
    restored, projector = smooth(*exchange(flat, first))
    return restored.reshape(TILE_ROWS, TILE_COLS, BANDS), projector


def solution(mesh):
    return jax.shard_map(
        body,
        mesh=mesh,
        in_specs=(P("narrow", "wide", None),),
        out_specs=(P("narrow", "wide", None), P()),
        check_vma=False,
    )
```
